128 devices in a mesh: dp: 16 (over z_lo, x, core), node: 8 (over y, z_hi).
Axes of the slice: x: 4, y: 4, z: 4 (z_hi: 2, z_lo: 2; z = z_hi * 2 + z_lo), core: 2. Of those that a mesh axis runs over, the one named last changes fastest.
Arguments:
- tokens: bfloat16 [65536, 8192], P(('dp', 'node')), may hold values from -24 to 24
- weight_codes: bfloat16 [8192, 1024], P('node'), may hold values from -4 to 4
- block_scales: float32 [64, 8], P('node'), may hold values from 0.0055242716 to 0.022097087
- value_grad: bfloat16 [65536, 1024], P(('dp', 'node')), may hold values from -6 to 6
Outputs:
- values: bfloat16 [65536, 1024], P(('dp', 'node'))
- input_grad: bfloat16 [65536, 8192], P(('dp', 'node'))
- weight_grad: float32 [8192, 1024], P(('dp', 'node'))
The draws below stay inside these ranges and needn't reach their ends.
All inputs are finite; a program needn't handle non-finite values.
Results may differ from the reference program's by a relative error of at most 0.0055.
Values may be sent and summed in bfloat16 or wider, within the bound.
No kernel may reach another device: no remote copies, remote signals or barrier semaphores. Data moves between devices by JAX's collectives and lax.ppermute only.
A program may use at most 192 MiB of HBM per device.

```python
import math
import jax
import jax.numpy as jnp
from jax import lax

D = 8192
KVW = 1024
BLK = 128
TOK_DEV = 512
TOKENS = 65536


def raised(entries, key, source, target, parts, factor):
    def block_of(dim):
        return (jnp.arange(entries.shape[dim]) // (entries.shape[dim] // parts)).reshape((-1,) + (1,) * (entries.ndim - 1 - dim))

    first = jax.random.permutation(key, parts)[block_of(target)]
    other_side = (block_of(target) + parts // 2) % parts
    return jnp.where((block_of(source) == first) | (block_of(source) == other_side), factor * entries, entries)


def block_levels(rng, dims, shards, low, high):
    loudness = 1.0
    for dim, shards_of in shards:
        steps = jax.random.uniform(jax.random.fold_in(jax.random.fold_in(rng, 6), dim), (shards_of,), jnp.float32, low / len(shards), high / len(shards))
        loudness = loudness * jnp.repeat(jnp.exp(steps), dims[dim] // shards_of).reshape((-1,) + (1,) * (len(dims) - 1 - dim))
    return loudness


def bell_draw(own_key, shape, spread, most, cuts=(), held_as=jnp.bfloat16):
    array = spread * jax.random.normal(own_key, shape, jnp.float32)
    if cuts:
        array = array * block_levels(own_key, shape, cuts, -0.22, 0.18)
    return jnp.clip(array, -most, most).astype(held_as)


def gaussian_with(own_key, dims, deviation, reach, shards, heavy, kind=jnp.bfloat16):
    array = deviation * jax.random.normal(own_key, dims, jnp.float32)
    if shards:
        array = array * block_levels(own_key, dims, shards, -0.22, 0.18)
    return jnp.clip(raised(array, jax.random.fold_in(own_key, 3), *heavy), -reach, reach).astype(kind)


def setup_inputs(seed: int = 0) -> dict:
    streams_of = jax.random.split(jax.random.key(seed), 5)
    return {
        "tokens": gaussian_with(streams_of[0], (TOKENS, D), 1.0, 24.0, ((0, 128),), (0, 1, 128, 5.5)),
        "weight_codes": bell_draw(streams_of[1], (D, KVW), 1.0, 4.0, ((0, 8),)),
        "block_scales": jnp.clip(jnp.exp(math.log(0.022097087) - 1.3862944 * jax.random.uniform(streams_of[2], (D // BLK, KVW // BLK), jnp.float32) ** block_levels(streams_of[2], (D // BLK, KVW // BLK), ((0, 8),), -0.2, 0.2)), 0.0055242716, 0.022097087),
        "value_grad": bell_draw(streams_of[3], (TOKENS, KVW), 1.0, 6.0, ((0, 128),)),
    }


def reference(tokens, weight_codes, block_scales, value_grad):
    row_blocks = D // BLK
    col_blocks = KVW // BLK
    scaled = weight_codes.astype(jnp.float32).reshape(row_blocks, BLK, col_blocks, BLK) * block_scales[:, None, :, None]
    weight = scaled.reshape(D, KVW).astype(jnp.bfloat16)
    values = jnp.dot(tokens, weight, preferred_element_type=jnp.float32).astype(jnp.bfloat16)
    input_grad = jnp.dot(value_grad, weight.T, preferred_element_type=jnp.float32).astype(jnp.bfloat16)
    loss_scale = TOKENS ** -0.5

    def add_group(running, block_pair):
        token_block, grad_block = block_pair
        product = lax.dot_general(token_block, grad_block, (((0,), (0,)), ((), ())), preferred_element_type=jnp.float32)
        grad_term = (product * loss_scale).astype(jnp.bfloat16)
        return running + grad_term.astype(jnp.float32), None

    start = jnp.zeros((D, KVW), jnp.float32)
    groups = TOKENS // TOK_DEV
    weight_grad, _ = lax.scan(add_group, start, (tokens.reshape(groups, TOK_DEV, D), value_grad.reshape(groups, TOK_DEV, KVW)))
    return values, input_grad, weight_grad
```

```python
import jax
import jax.numpy as jnp
import numpy as np
from jax import lax
from jax.experimental import pallas as pl
from jax.experimental.pallas import tpu as pltpu
from jax.sharding import Mesh
from jax.sharding import PartitionSpec as P


AXES = ("zl", "x", "c", "y", "zh")
BF = jnp.bfloat16
F32 = jnp.float32
CA, CB, CC = 384, 384, 256


def rank(x, y, z, c):
    return ((((z % 2) * 4 + x % 4) * 2 + c) * 4 + y % 4) * 2 + (z % 4) // 2


def hop(a, dx=0, dy=0, dz=0, dc=0):
    pairs = [
        (rank(x, y, z, c), rank(x + dx, y + dy, (z + dz) % 4, c ^ dc))
        for x in range(4)
        for y in range(4)
        for z in range(4)
        for c in range(2)
    ]
    return lax.ppermute(a, AXES, pairs)


def cost(flops, nbytes):
    return pl.CostEstimate(flops=flops, bytes_accessed=nbytes, transcendentals=0)


def dot(a, b, dims):
    return lax.dot_general(a, b, (dims, ((), ())), preferred_element_type=F32)


def other_half(pos, tokens):
    rows, cols = tokens.shape

    def body(pos_ref, t_ref, o_ref):
        o_ref[...] = t_ref[...]

    return pl.pallas_call(
        body,
        grid_spec=pltpu.PrefetchScalarGridSpec(
            num_scalar_prefetch=1,
            grid=(8,),
            in_specs=[pl.BlockSpec((rows, cols // 16), lambda i, p: (0, 2 * i + 1 - p[2]))],
            out_specs=pl.BlockSpec((rows, cols // 16), lambda i, p: (0, i)),
        ),
        out_shape=jax.ShapeDtypeStruct((rows, cols // 2), BF),
        cost_estimate=cost(0, 2 * rows * cols),
        name="other_half",
    )(pos, tokens)


def grad_call(body, grid, slab, col_block, width, out_shape, out_specs, scratch, name, scale, args):
    pos, tokens, tokens2, vg, vg2 = args
    rows = tokens.shape[0]

    def full(pos_ref, t_ref, t2_ref, v_ref, v2_ref, *rest):
        r = dot(t_ref[...], v_ref[...], ((0,), (0,))) + dot(t2_ref[...], v2_ref[...], ((0,), (0,)))
        body(pos_ref, r * scale, *rest)

    return pl.pallas_call(
        full,
        grid_spec=pltpu.PrefetchScalarGridSpec(
            num_scalar_prefetch=1,
            grid=grid,
            in_specs=[
                pl.BlockSpec((rows, 512), lambda i, j, p: (0, 2 * slab(i, j, p) + p[2])),
                pl.BlockSpec((rows, 512), lambda i, j, p: (0, slab(i, j, p))),
                pl.BlockSpec((rows, width), lambda i, j, p: (0, col_block)),
                pl.BlockSpec((rows, width), lambda i, j, p: (0, col_block)),
            ],
            out_specs=out_specs,
            scratch_shapes=scratch,
        ),
        out_shape=out_shape,
        cost_estimate=cost(4 * rows * 4096 * width, 4 * rows * 4096 + 2 * 4096 * width),
        name=name,
    )(pos, tokens, tokens2, vg, vg2)


def grad_a(scale, *args):
    def body(pos_ref, r, *outs):
        for k in range(4):

            @pl.when(pl.program_id(0) == k)
            def _():
                outs[k][0] = r.astype(BF)

    def index(k):
        return lambda d, zl, p: (jnp.where(d == k, zl, jnp.where(d < k, 0, 1)), 0, 0)

    return grad_call(
        body,
        (4, 2),
        lambda d, zl, p: zl * 4 + (p[1] + d) % 4,
        0,
        CA,
        [jax.ShapeDtypeStruct((2, 512, CA), BF)] * 4,
        [pl.BlockSpec((1, 512, CA), index(k)) for k in range(4)],
        [],
        "grad_a",
        scale,
        args,
    )


def grad_b(scale, *args):
    def body(pos_ref, r, *rest):
        outs, scr = rest[:4], rest[4]
        scr[...] = r.astype(BF).reshape(4, 128, CB)
        for k in range(4):
            outs[k][0] = scr[(pos_ref[3] + k) % 4]

    return grad_call(
        body,
        (2, 4),
        lambda zl, x, p: zl * 4 + x,
        1,
        CB,
        [jax.ShapeDtypeStruct((8, 128, CB), BF)] * 4,
        [pl.BlockSpec((1, 128, CB), lambda zl, x, p: (zl * 4 + x, 0, 0))] * 4,
        [pltpu.VMEM((4, 128, CB), BF)],
        "grad_b",
        scale,
        args,
    )


def grad_c(scale, *args):
    def body(pos_ref, r, *rest):
        outs, scr = rest[:4], rest[4]
        scr[...] = r.astype(BF).reshape(8, 64, CC)
        z = pos_ref[4] * 2 + pos_ref[0]
        for e in range(2):

            @pl.when(pl.program_id(0) == e)
            def _():
                zh = ((z + e) % 4) // 2
                for y in range(4):
                    outs[e][0, y] = scr[2 * y + zh]
                    outs[e + 2][0, y] = scr[2 * y + 1 - zh]

    def index(k):
        if k % 2 == 0:
            return lambda e, x, p: (jnp.where(e == 0, x, 3), 0, 0, 0)
        return lambda e, x, p: (jnp.where(e == 0, 0, x), 0, 0, 0)

    return grad_call(
        body,
        (2, 4),
        lambda e, x, p: ((p[0] + e) % 2) * 4 + x,
        3,
        CC,
        [jax.ShapeDtypeStruct((4, 4, 64, CC), BF)] * 4,
        [pl.BlockSpec((1, 4, 64, CC), index(k)) for k in range(4)],
        [pltpu.VMEM((8, 64, CC), BF)],
        "grad_c",
        scale,
        args,
    )


SMEM = pl.BlockSpec(memory_space=pltpu.SMEM)
VMEM = pl.BlockSpec(memory_space=pltpu.VMEM)


def small_call(body, name, pos, ins, outs):
    nbytes = sum(a.size * a.dtype.itemsize for a in list(ins) + list(outs))
    return pl.pallas_call(
        body,
        in_specs=[SMEM] + [VMEM] * len(ins),
        out_specs=[VMEM] * len(outs),
        out_shape=outs,
        cost_estimate=cost(nbytes, nbytes),
        name=name,
    )(pos, *ins)


def total(refs, index):
    s = refs[0][index].astype(F32)
    for r in refs[1:]:
        s = s + r[index].astype(F32)
    return s


def second_a(pos, parts):
    parts = [p.reshape(2, 4, 2, 64, CA) for p in parts]

    def body(pos_ref, *refs):
        ins, outs = refs[:4], refs[4:]
        for k in range(4):
            y = (pos_ref[3] + k) % 4
            for zl in range(2):
                for zh in range(2):
                    outs[k][2 * zl + zh] = total(ins, (zl, y, zh)).astype(BF)

    return small_call(body, "second_a", pos, parts, [jax.ShapeDtypeStruct((4, 64, CA), BF)] * 4)


def second_bc(pos, parts_b, parts_c):
    parts_b = [p.reshape(2, 4, 2, 64, CB) for p in parts_b]

    def body(pos_ref, *refs):
        b, c, outs = refs[:4], refs[4:8], refs[8:]
        for k in range(4):
            x = (pos_ref[1] + k) % 4
            for zl in range(2):
                for zh in range(2):
                    outs[k][2 * zl + zh, :, :CB] = total(b, (zl, x, zh)).astype(BF)
            for y in range(4):
                outs[k][y, :, CB:] = total(c, (x, y)).astype(BF)

    return small_call(
        body, "second_bc", pos, list(parts_b) + list(parts_c), [jax.ShapeDtypeStruct((4, 64, CB + CC), BF)] * 4
    )


def third(pos, parts_a, parts_bc):
    def body(pos_ref, *refs):
        a, bc, ab, c = refs[:4], refs[4:8], refs[8:12], refs[12:]
        z0 = pos_ref[4] * 2 + pos_ref[0]
        for k in range(4):
            z = (z0 + k) % 4
            block = (z % 2) * 2 + z // 2
            ab[k][:, :CA] = total(a, (block,)).astype(BF)
            ab[k][:, CA:] = total(bc, (block, slice(None), slice(0, CB))).astype(BF)
            y = (pos_ref[3] + k) % 4
            c[k][...] = total(bc, (y, slice(None), slice(CB, CB + CC))).astype(BF)

    outs = small_call(
        body,
        "third",
        pos,
        list(parts_a) + list(parts_bc),
        [jax.ShapeDtypeStruct((64, CA + CB), BF)] * 4 + [jax.ShapeDtypeStruct((64, CC), BF)] * 4,
    )
    return outs[:4], outs[4:]


def last(pos, parts_ab, parts_c):
    def body(pos_ref, *refs):
        ab, c, out = refs[:4], refs[4:8], refs[8]
        out[:, : CA + CB] = total(ab, ...)
        out[:, CA + CB :] = total(c, ...)

    return small_call(
        body, "last", pos, list(parts_ab) + list(parts_c), [jax.ShapeDtypeStruct((64, CA + CB + CC), F32)]
    )[0]


def exchange(parts, axis):
    return [parts[0]] + [hop(parts[k], **{axis: k}) for k in (1, 3, 2)]


def weight_call(tokens, vg, weight):
    rows, width = tokens.shape
    cols = vg.shape[1]
    step = 512
    steps = width // step

    def body(t_ref, v_ref, w_ref, val_ref, ig_ref, acc):
        i = pl.program_id(0)
        w = w_ref[...]
        ig_ref[...] = dot(v_ref[...], w, ((1,), (1,))).astype(BF)
        part = dot(t_ref[...], w, ((1,), (0,)))

        @pl.when(i == 0)
        def _():
            acc[...] = part

        @pl.when(i > 0)
        def _():
            acc[...] += part

        @pl.when(i == steps - 1)
        def _():
            val_ref[...] = acc[...].astype(BF)

    return pl.pallas_call(
        body,
        grid=(steps,),
        in_specs=[
            pl.BlockSpec((rows, step), lambda i: (0, i)),
            pl.BlockSpec((rows, cols), lambda i: (0, 0)),
            pl.BlockSpec((step, cols), lambda i: (i, 0)),
        ],
        out_specs=[pl.BlockSpec((rows, cols), lambda i: (0, 0)), pl.BlockSpec((rows, step), lambda i: (0, i))],
        scratch_shapes=[pltpu.VMEM((rows, cols), F32)],
        out_shape=[jax.ShapeDtypeStruct((rows, cols), BF), jax.ShapeDtypeStruct((rows, width), BF)],
        cost_estimate=cost(4 * rows * width * cols, 4 * rows * width + 2 * width * cols),
        name="weight_products",
    )(tokens, vg, weight)


def shards(tokens, weight_codes, block_scales, value_grad):
    rows = tokens.shape[0]
    scale = (rows * 128) ** (-0.5)
    here = lax.axis_index(AXES)
    pos = (here // jnp.array([64, 16, 8, 2, 1], jnp.int32)) % jnp.array([2, 4, 2, 4, 2], jnp.int32)

    dp = here // 8
    piece = weight_codes.shape[0] // 16
    codes = lax.dynamic_slice_in_dim(weight_codes, dp * piece, piece, 0)
    block = lax.dynamic_slice_in_dim(block_scales, dp * piece // 128, 1, 0)
    local = (codes.astype(F32).reshape(piece, 8, 128) * block[:, :, None]).reshape(piece, 1024).astype(BF)
    weight = lax.all_gather(local, ("y", "zh", "zl", "x", "c"), axis=0, tiled=True)

    vg2 = hop(value_grad, dc=1)
    tokens2 = hop(other_half(pos, tokens), dc=1)
    args = (pos, tokens, tokens2, value_grad, vg2)
    a1 = exchange(grad_a(scale, *args), "dx")
    b1 = exchange(grad_b(scale, *args), "dy")
    c1 = exchange(grad_c(scale, *args), "dz")
    a2 = exchange(second_a(pos, a1), "dy")
    bc2 = exchange(second_bc(pos, b1, c1), "dx")
    ab3, c3 = third(pos, a2, bc2)
    weight_grad = last(pos, exchange(ab3, "dz"), exchange(c3, "dy"))

    values, input_grad = weight_call(tokens, value_grad, weight)
    return values, input_grad, weight_grad


def solution(mesh):
    fine = Mesh(np.asarray(mesh.devices).reshape(2, 4, 2, 4, 2), AXES)
    nodes = ("y", "zh")
    in_specs = (P(AXES, None), P(nodes, None), P(nodes, None), P(AXES, None))
    out_specs = (P(AXES, None), P(AXES, None), P(AXES, None))
    return jax.shard_map(shards, mesh=fine, in_specs=in_specs, out_specs=out_specs, check_vma=False)
```

```python
import jax
import jax.numpy as jnp
import numpy as np
from jax import lax
from jax.experimental import pallas as pl
from jax.experimental.pallas import tpu as pltpu
from jax.sharding import Mesh
from jax.sharding import PartitionSpec as P


AXES = ("zl", "x", "c", "y", "zh")
BF = jnp.bfloat16
F32 = jnp.float32
BIG, SMALL = 768, 256
SMEM = pl.BlockSpec(memory_space=pltpu.SMEM)
VMEM = pl.BlockSpec(memory_space=pltpu.VMEM)
ANY = pl.BlockSpec(memory_space=pl.ANY)


def rank(x, y, z, c):
    return ((((z % 2) * 4 + x % 4) * 2 + c) * 4 + y % 4) * 2 + (z % 4) // 2


def hop(a, target):
    places = [(x, y, z, c) for x in range(4) for y in range(4) for z in range(4) for c in range(2)]
    return lax.ppermute(a, AXES, [(rank(*p), rank(*target(*p))) for p in places])


def swap(a):
    return hop(a, lambda x, y, z, c: (x, y, z, 1 - c))


def along_u(k):
    return lambda x, y, z, c: (x + k, y, z, c) if c == 0 else (x, y + k, z, c)


def along_v(k):
    return lambda x, y, z, c: (x, y + k, z, c) if c == 0 else (x + k, y, z, c)


def along_z(k):
    return lambda x, y, z, c: (x, y, (z + k) % 4, c)


def exchange(parts, along):
    return [parts[0]] + [hop(parts[k], along(k)) for k in (1, 3, 2)]


def place(pos_ref):
    p = pos_ref[0]
    zl, x, c, y, zh = p >> 6, (p >> 4) & 3, (p >> 3) & 1, (p >> 1) & 3, p & 1
    u = jnp.where(c == 0, x, y)
    v = jnp.where(c == 0, y, x)
    return x, y, zh * 2 + zl, c, u, v


def cost(flops, nbytes):
    return pl.CostEstimate(flops=flops, bytes_accessed=nbytes, transcendentals=0)


def dot(a, b, dims):
    return lax.dot_general(a, b, (dims, ((), ())), preferred_element_type=F32)


def flip(vg):
    def body(v_ref, o_ref):
        o_ref[...] = v_ref[...].T

    return pl.pallas_call(
        body,
        out_shape=jax.ShapeDtypeStruct(vg.shape[::-1], BF),
        in_specs=[VMEM],
        out_specs=VMEM,
        cost_estimate=cost(0, 4 * vg.size),
        name="flip",
    )(vg)


def other_half(pos, tokens, half):
    rows = tokens.shape[0]

    def body(pos_ref, *refs):
        for k in range(4):
            refs[4][:, 512 * k : 512 * k + 512] = refs[k][...]

    def index(k):
        return lambda i, p: (0, 2 * (4 * half + k) + 1 - ((p[0] >> 3) & 1))

    return pl.pallas_call(
        body,
        grid_spec=pltpu.PrefetchScalarGridSpec(
            num_scalar_prefetch=1,
            grid=(1,),
            in_specs=[pl.BlockSpec((rows, 512), index(k)) for k in range(4)],
            out_specs=pl.BlockSpec((rows, 2048), lambda i, p: (0, 0)),
        ),
        out_shape=jax.ShapeDtypeStruct((rows, 2048), BF),
        cost_estimate=cost(0, 8 * rows * 1024),
        name="other_half",
    )(pos, *[tokens] * 4)


def low_lanes(a, b):
    lane = lax.broadcasted_iota(jnp.int32, a.shape, 1)
    return jnp.where(lane < 64, a, pltpu.roll(b, 64, 1))


def high_lanes(a, b):
    lane = lax.broadcasted_iota(jnp.int32, a.shape, 1)
    return jnp.where(lane < 64, pltpu.roll(a, 64, 1), b)


def grad_call(send, width, row_block, name, scale, pos, tokens, first, second, vgt, vgt2):
    rows = tokens.shape[0]

    def body(pos_ref, t0, t1, h0, h1, v, v2, *rest):
        outs, scr, sem = rest[:4], rest[4], rest[5]
        i = pl.program_id(0)

        def products(received):
            return [
                (
                    dot(v[...], t[...], ((1,), (0,)))
                    + dot(v2[...], received[:, 512 * k : 512 * k + 512], ((1,), (0,)))
                )
                * scale
                for k, t in enumerate((t0, t1))
            ]

        def put(slot, block, k, index):
            scr[slot] = block.astype(BF)
            for j in range(4):

                @pl.when(k == j)
                def _():
                    pltpu.make_async_copy(scr.at[slot], outs[j].at[index], sem.at[8 * j + index]).start()

        @pl.when(i < 2)
        def _():
            send(place(pos_ref), i, products(h0), put)

        @pl.when(i >= 2)
        def _():
            send(place(pos_ref), i, products(h1), put)

        @pl.when(i == 3)
        def _():
            for j in range(4):
                for index in range(8):
                    pltpu.make_async_copy(scr.at[0], outs[j].at[index], sem.at[8 * j + index]).wait()

    def slab(k):
        return lambda i, p: (0, 2 * (2 * i + k) + ((p[0] >> 3) & 1))

    return pl.pallas_call(
        body,
        grid_spec=pltpu.PrefetchScalarGridSpec(
            num_scalar_prefetch=1,
            grid=(4,),
            in_specs=[
                pl.BlockSpec((rows, 512), slab(0)),
                pl.BlockSpec((rows, 512), slab(1)),
                pl.BlockSpec((rows, 1024), lambda i, p: (0, jnp.minimum(i, 1))),
                pl.BlockSpec((rows, 1024), lambda i, p: (0, jnp.maximum(i - 2, 0))),
                pl.BlockSpec((width, rows), lambda i, p: (row_block, 0)),
                pl.BlockSpec((width, rows), lambda i, p: (row_block, 0)),
            ],
            out_specs=[ANY] * 4,
            scratch_shapes=[pltpu.VMEM((32, width, 128), BF), pltpu.SemaphoreType.DMA((32,))],
        ),
        out_shape=[jax.ShapeDtypeStruct((8, width, 128), BF)] * 4,
        cost_estimate=cost(4 * rows * 4096 * width, 4 * rows * 4096 + 2 * 4096 * width),
        name=name,
    )(pos, tokens, tokens, first, second, vgt, vgt2)


def grad_big(*args):
    def send(here, i, products, put):
        x, y, z, c, u, v = here
        zl = i // 2
        for t in range(2):
            column = 2 * (i % 2) + t
            for j in range(4):
                k = jnp.where(c == 0, column - x, j - y) & 3
                index = zl * 4 + jnp.where(c == 0, j, column)
                put((2 * i + t) * 4 + j, products[t][:, 128 * j : 128 * j + 128], k, index)

    return grad_call(send, BIG, 0, "grad_big", *args)


def grad_small(*args):
    def send(here, i, products, put):
        x, y, z, c, u, v = here
        zl, h = i // 2, i % 2
        lanes = [[p[:, 128 * j : 128 * j + 128] for j in range(4)] for p in products]
        for zh, pick in enumerate((low_lanes, high_lanes)):
            k = (zh * 2 + zl - z) & 3

            @pl.when(c == 0)
            def _():
                for j in range(4):
                    put((2 * i + zh) * 4 + j, pick(lanes[0][j], lanes[1][j]), k, 2 * j + h)

            @pl.when(c == 1)
            def _():
                for t in range(2):
                    for g in range(2):
                        block = pick(lanes[t][2 * g], lanes[t][2 * g + 1])
                        put((2 * i + zh) * 4 + 2 * t + g, block, k, 2 * (2 * h + t) + g)

    return grad_call(send, SMALL, 3, "grad_small", *args)


def small_call(body, name, pos, ins, outs, scratch=()):
    nbytes = sum(a.size * a.dtype.itemsize for a in list(ins) + list(outs))
    return pl.pallas_call(
        body,
        in_specs=[SMEM] + [VMEM] * len(ins),
        out_specs=[VMEM] * len(outs),
        out_shape=outs,
        scratch_shapes=list(scratch),
        cost_estimate=cost(nbytes, nbytes),
        name=name,
    )(pos, *ins)


def total(refs, index):
    s = refs[0][index].astype(F32)
    for r in refs[1:]:
        s = s + r[index].astype(F32)
    return s


def second(pos, big, small):
    def body(pos_ref, *refs):
        b, s, outs = refs[:4], refs[4:8], refs[8:]
        v0 = place(pos_ref)[5]
        for k in range(4):
            v = (v0 + k) & 3
            for h in range(2):
                outs[k][h, :BIG] = total(b, (4 * h + v,)).astype(BF)
                outs[k][h, BIG:] = total(s, (2 * v + h,)).astype(BF)

    outs = [jax.ShapeDtypeStruct((2, BIG + SMALL, 128), BF)] * 4
    return small_call(body, "second", pos, list(big) + list(small), outs)


def third(pos, parts):
    def body(pos_ref, *refs):
        ins, big, small, scr_b, scr_s = refs[:4], refs[4:8], refs[8:12], refs[12], refs[13]
        x, y, z0, c, u, v = place(pos_ref)
        for h in range(2):
            a, b = total(ins, (h, slice(0, BIG // 2))), total(ins, (h, slice(BIG // 2, BIG)))
            scr_b[2 * h] = low_lanes(a, b).astype(BF)
            scr_b[2 * h + 1] = high_lanes(a, b).astype(BF)
            middle = BIG + SMALL // 2
            a, b = total(ins, (h, slice(BIG, middle))), total(ins, (h, slice(middle, BIG + SMALL)))
            scr_s[2 * h] = low_lanes(a, b).astype(BF)
            scr_s[2 * h + 1] = high_lanes(a, b).astype(BF)
        for k in range(4):
            z = (z0 + k) & 3
            big[k][...] = scr_b[(z & 1) * 2 + (z >> 1)]
            small[k][...] = scr_s[(u + k) & 3]

    outs = [jax.ShapeDtypeStruct((BIG // 2, 128), BF)] * 4 + [jax.ShapeDtypeStruct((SMALL // 2, 128), BF)] * 4
    scratch = [pltpu.VMEM((4, BIG // 2, 128), BF), pltpu.VMEM((4, SMALL // 2, 128), BF)]
    outs = small_call(body, "third", pos, parts, outs, scratch)
    return outs[:4], outs[4:]


def last(pos, big, small):
    def body(pos_ref, *refs):
        b, s, out = refs[:4], refs[4:8], refs[8]
        r = total(b, ...).T
        out[:, : BIG // 2] = r[:64]
        out[:, BIG // 2 : BIG] = r[64:]
        r = total(s, ...).T
        out[:, BIG : BIG + SMALL // 2] = r[:64]
        out[:, BIG + SMALL // 2 :] = r[64:]

    return small_call(
        body, "last", pos, list(big) + list(small), [jax.ShapeDtypeStruct((64, BIG + SMALL), F32)]
    )[0]


def weight_call(tokens, vg, weight, part, parts, carried):
    rows, width = tokens.shape
    cols = vg.shape[1]
    step = 1024
    steps = width // step // parts
    start, end = part == 0, part == parts - 1

    def body(t_ref, v_ref, w_ref, *refs):
        val_ref, ig_ref, acc = refs[-3:]
        i = pl.program_id(0)
        w = w_ref[...]
        ig_ref[...] = dot(v_ref[...], w, ((1,), (1,))).astype(BF)
        product = dot(t_ref[...], w, ((1,), (0,)))

        @pl.when(i == 0)
        def _():
            acc[...] = product if start else refs[0][...] + product

        @pl.when(i > 0)
        def _():
            acc[...] += product

        @pl.when(i == steps - 1)
        def _():
            val_ref[...] = acc[...].astype(val_ref.dtype)

    first = part * steps
    in_specs = [
        pl.BlockSpec((rows, step), lambda i: (0, first + i)),
        pl.BlockSpec((rows, cols), lambda i: (0, 0)),
        pl.BlockSpec((step, cols), lambda i: (first + i, 0)),
    ]
    if not start:
        in_specs += [pl.BlockSpec((rows, cols), lambda i: (0, 0)), ANY]
    return pl.pallas_call(
        body,
        grid=(steps,),
        in_specs=in_specs,
        out_specs=[
            pl.BlockSpec((rows, cols), lambda i: (0, 0)),
            pl.BlockSpec((rows, step), lambda i: (0, first + i)),
        ],
        scratch_shapes=[pltpu.VMEM((rows, cols), F32)],
        out_shape=[jax.ShapeDtypeStruct((rows, cols), BF if end else F32), jax.ShapeDtypeStruct((rows, width), BF)],
        input_output_aliases={} if start else {4: 1},
        cost_estimate=cost(4 * rows * width * cols // parts, (4 * rows * width + 2 * width * cols) // parts),
        name="weight_products",
    )(tokens, vg, weight, *carried)


def shards(tokens, weight_codes, block_scales, value_grad):
    rows = tokens.shape[0]
    scale = (rows * 128) ** (-0.5)
    here = lax.axis_index(AXES)
    pos = here.reshape(1)

    dp = here // 8
    piece = weight_codes.shape[0] // 16
    codes = lax.dynamic_slice_in_dim(weight_codes, dp * piece, piece, 0)
    block = lax.dynamic_slice_in_dim(block_scales, dp * piece // 128, 1, 0)
    local = (codes.astype(F32).reshape(piece, 8, 128) * block[:, :, None]).reshape(piece, 1024).astype(BF)
    weight = lax.all_gather(local, ("y", "zh", "zl", "x", "c"), axis=0, tiled=True)

    first = swap(other_half(pos, tokens, 0))
    vgt = flip(value_grad)
    vgt2 = swap(vgt)
    second_half = swap(other_half(pos, tokens, 1))
    args = (scale, pos, tokens, first, second_half, vgt, vgt2)
    big = exchange(grad_big(*args), along_u)
    small = exchange(grad_small(*args), along_z)
    parts = exchange(second(pos, big, small), along_v)
    carried = weight_call(tokens, value_grad, weight, 0, 2, ())
    parts, carried = lax.optimization_barrier((parts, carried))
    big, small = third(pos, parts)
    big, small = exchange(big, along_z), exchange(small, along_u)
    values, input_grad = weight_call(tokens, value_grad, weight, 1, 2, carried)
    big, small, values, input_grad = lax.optimization_barrier((big, small, values, input_grad))
    weight_grad = last(pos, big, small)
    return values, input_grad, weight_grad


def solution(mesh):
    fine = Mesh(np.asarray(mesh.devices).reshape(2, 4, 2, 4, 2), AXES)
    nodes = ("y", "zh")
    in_specs = (P(AXES, None), P(nodes, None), P(nodes, None), P(AXES, None))
    out_specs = (P(AXES, None), P(AXES, None), P(AXES, None))
    return jax.shard_map(shards, mesh=fine, in_specs=in_specs, out_specs=out_specs, check_vma=False)
```
